128 devices in a mesh: ctx: 8 (over y_lo, z), head: 16 (over y_hi, x, core).
Axes of the slice: x: 4, y: 4 (y_hi: 2, y_lo: 2; y = y_hi * 2 + y_lo), z: 4, core: 2. Of those that a mesh axis runs over, the one named last changes fastest.
Arguments:
- queries: bfloat16 [8192, 24576], P('ctx', 'head'), may hold values from -110 to 110
- latent_kv: bfloat16 [8192, 576], P('ctx'), may hold values from -6 to 6
- w_uk: bfloat16 [128, 512, 128], P('head'), may hold values from -0.25 to 0.25
- w_uv: bfloat16 [128, 512, 128], P('head'), may hold values from -0.25 to 0.25
- grad_out: bfloat16 [8192, 16384], P('ctx', 'head'), may hold values from -48 to 48
Outputs:
- grad_queries: bfloat16 [8192, 24576], P('ctx', 'head')
- grad_latent: float32 [8192, 576], P(('ctx', 'head'))
The draws below stay inside these ranges and needn't reach their ends.
All inputs are finite; a program needn't handle non-finite values.
Results may differ from the reference program's by a relative error of at most 0.013.
Values may be sent and summed in bfloat16 or wider, within the bound.
No kernel may reach another device: no remote copies, remote signals or barrier semaphores. Data moves between devices by JAX's collectives and lax.ppermute only.
A program may use at most 128 MiB of HBM per device.

```python
import jax
import jax.numpy as jnp
from jax import lax

HEADS = 128
DN = 128
DR = 64
DV = 128
DL = 512
W = 512
TOKENS = 8192


def latent_rows_draw(key):
    base = jax.random.fold_in(key, 11)
    latent = jnp.clip(jax.random.normal(base, (TOKENS, DL + DR), jnp.float32), -6.0, 6.0)
    return latent


def draw_latent_kv(key, part):
    return latent_rows_draw(key).astype(jnp.bfloat16)


def draw_queries(key, part):
    base = jax.random.fold_in(key, 23)
    random_example = jnp.clip(jax.random.normal(base, (TOKENS, HEADS, DN + DR), jnp.float32), -6.0, 6.0)
    return random_example.reshape(TOKENS, HEADS * (DN + DR)).astype(jnp.bfloat16)


def steps_of(stream_key, shape, cuts, low, largest):
    def one(position, shards_of):
        draws = jax.random.uniform(jax.random.fold_in(jax.random.fold_in(stream_key, 6), position), (shards_of,), jnp.float32, low / len(cuts), largest / len(cuts))
        return jnp.repeat(jnp.exp(draws), shape[position] // shards_of).reshape((-1,) + (1,) * (len(shape) - position - 1))

    gain = one(*cuts[0])
    for cut in cuts[1:]:
        gain = gain * one(*cut)
    return gain


def bell_draw(rng, shape, deviation, reach, shards=(), kind=jnp.bfloat16):
    array = deviation * jax.random.normal(rng, shape, jnp.float32)
    if shards:
        array = array * steps_of(rng, shape, shards, -0.22, 0.18)
    return jnp.clip(array, -reach, reach).astype(kind)


def setup_inputs(seed: int = 0) -> dict:
    streams_of = jax.random.split(jax.random.key(seed), 6)
    queries = draw_queries(jax.random.fold_in(streams_of[5], 71), 0)
    latent_kv = draw_latent_kv(jax.random.fold_in(streams_of[5], 71), 0)
    w_uk = bell_draw(streams_of[2], (HEADS, DL, DN), DL ** -0.5, 0.25, ((0, 16),))
    w_uv = bell_draw(streams_of[3], (HEADS, DL, DV), DL ** -0.5, 0.25, ((0, 16),))
    grad_out = bell_draw(streams_of[4], (TOKENS, HEADS * DV), 8.0, 48.0, ((0, 8), (1, 16)))
    return dict(queries=queries, latent_kv=latent_kv, w_uk=w_uk, w_uv=w_uv, grad_out=grad_out)


def windows(array_in, block_count):
    zeros_pad = jnp.zeros((W,) + array_in.shape[1:], array_in.dtype)
    padded = jnp.concatenate([zeros_pad, array_in], axis=0)
    lower_part = padded[:-W].reshape((block_count, W) + array_in.shape[1:])
    upper_part = padded[W:].reshape((block_count, W) + array_in.shape[1:])
    return jnp.concatenate([lower_part, upper_part], axis=1)


def fold_window_back(window_terms, row_total_count):
    tail_shape = window_terms.shape[2:]
    lower_part = window_terms[:, :W].reshape((row_total_count,) + tail_shape)
    upper_part = window_terms[:, W:].reshape((row_total_count,) + tail_shape)
    shifted = jnp.concatenate([lower_part[W:], jnp.zeros((W,) + tail_shape, jnp.float32)], axis=0)
    return upper_part + shifted


def reference(queries, latent_kv, w_uk, w_uv, grad_out):
    row_total_count = queries.shape[0]
    block_count = row_total_count // W
    query_dim = DN + DR
    score_scale = query_dim ** -0.5
    query_rows = queries.reshape(row_total_count, HEADS, query_dim)
    grad_rows = grad_out.reshape(row_total_count, HEADS, DV)
    latent_part = latent_kv[:, :DL]
    banded_positional_part = windows(latent_kv[:, DL:], block_count).astype(jnp.float32)
    lower_idx = jnp.arange(W)[:, None]
    upper_idx = jnp.arange(2 * W)[None, :]
    band = (upper_idx > lower_idx) & (upper_idx <= lower_idx + W)
    block_idx = jnp.arange(block_count)[:, None, None]
    allowed = band[None] & ((block_idx > 0) | (upper_idx[None] >= W))

    def head_step(accum, head):
        keys_nope = jnp.dot(latent_part, w_uk[head], preferred_element_type=jnp.float32).astype(jnp.bfloat16)
        values = jnp.dot(latent_part, w_uv[head], preferred_element_type=jnp.float32).astype(jnp.bfloat16)
        windowed_keys = windows(keys_nope, block_count).astype(jnp.float32)
        windowed_values = windows(values, block_count).astype(jnp.float32)
        query_head = query_rows[:, head].reshape(block_count, W, query_dim).astype(jnp.float32)
        query_unrotated = query_head[:, :, :DN]
        query_rotary = query_head[:, :, DN:]
        head_gradient = grad_rows[:, head].reshape(block_count, W, DV).astype(jnp.float32)
        logit_scores = jnp.einsum("rpm,rsm->rps", query_unrotated, windowed_keys) + jnp.einsum("zvp,zhp->zvh", query_rotary, banded_positional_part)
        logit_scores = jnp.where(allowed, logit_scores * score_scale, -jnp.inf)
        peak = jnp.max(logit_scores, axis=2, keepdims=True)
        expo = jnp.exp(logit_scores - peak)
        probs = expo / jnp.sum(expo, axis=2, keepdims=True)
        lowered_probabilities = lax.optimization_barrier(probs.astype(jnp.bfloat16)).astype(jnp.float32)
        attended_output = jnp.einsum("swa,sao->swo", lowered_probabilities, windowed_values)
        delta = jnp.sum(head_gradient * attended_output, axis=2)
        probability_gradient = jnp.einsum("olj,oaj->ola", head_gradient, windowed_values)
        similarity_derivative = probs * (probability_gradient - delta[:, :, None])
        similarity_derivative = lax.optimization_barrier(similarity_derivative.astype(jnp.bfloat16)).astype(jnp.float32)
        unrotated_gradient = jnp.einsum("fyg,fgr->fyr", similarity_derivative, windowed_keys)
        positional_request_derivative = jnp.einsum("zcg,zgy->zcy", similarity_derivative, banded_positional_part)
        grad_query = (jnp.concatenate([unrotated_gradient, positional_request_derivative], axis=2) * score_scale).astype(jnp.bfloat16)
        key_gradient = fold_window_back(jnp.einsum("fjg,fjl->fgl", similarity_derivative, query_unrotated) * score_scale, row_total_count)
        value_gradient = fold_window_back(jnp.einsum("ytn,ytc->ync", lowered_probabilities, head_gradient), row_total_count)
        rotary_gradient = fold_window_back(jnp.einsum("pyj,pyl->pjl", similarity_derivative, query_rotary) * score_scale, row_total_count)
        latent_grad = jnp.dot(key_gradient, w_uk[head].astype(jnp.float32).T, precision=lax.Precision.HIGHEST)
        latent_grad = latent_grad + jnp.dot(value_gradient, w_uv[head].astype(jnp.float32).T, precision=lax.Precision.HIGHEST)
        accum = accum + jnp.concatenate([latent_grad, rotary_gradient], axis=1)
        return accum, grad_query.reshape(row_total_count, query_dim)

    start_accum = jnp.zeros((row_total_count, DL + DR), jnp.float32)
    grad_latent, per_head = lax.scan(head_step, start_accum, jnp.arange(HEADS, dtype=jnp.int32))
    grad_queries = jnp.transpose(per_head, (1, 0, 2)).reshape(row_total_count, HEADS * query_dim)
    return grad_queries, grad_latent
```

```python
import functools
import math

import jax
import jax.numpy as jnp
from jax import lax
from jax.experimental import pallas as pl
from jax.experimental.pallas import tpu as pltpu
from jax.sharding import PartitionSpec as P

W = 512
T = 256
SPAN = T + W
HALF = 128
STEP = 64
NEG = -1e30
F32 = jnp.float32
BF16 = jnp.bfloat16


def nn(a, b):
    return lax.dot_general(a, b, (((1,), (0,)), ((), ())), preferred_element_type=F32)


def nt(a, b):
    return lax.dot_general(a, b, (((1,), (1,)), ((), ())), preferred_element_type=F32)


def tn(a, b):
    return lax.dot_general(a, b, (((0,), (0,)), ((), ())), preferred_element_type=F32)


def fold(x, op):
    return op(x.reshape(x.shape[0] // 8, 8, x.shape[1]), axis=0)


def tile_softmax(s_ref, dp_ref, p_ref, ds_ref, first, tile, scale):
    factor = scale * math.log2(math.e)
    lane = lax.broadcasted_iota(jnp.int32, (STEP, HALF), 1)
    sub = lax.broadcasted_iota(jnp.int32, (STEP, HALF), 0)
    for half in range(2):
        lo = half * HALF
        cols = slice(lo, lo + HALF)
        starts = range(lo, lo + W + HALF, STEP)
        peak = jnp.full((8, HALF), NEG, F32)
        for r0 in starts:
            x = s_ref[r0 : r0 + STEP, cols]
            changed = False
            if r0 < lo + HALF:
                x = jnp.where(sub + (r0 - lo) > lane, x, NEG)
                changed = True
            if r0 >= lo + W:
                x = jnp.where(sub + (r0 - lo - W) <= lane, x, NEG)
                changed = True
            if r0 < W:
                bias = jnp.where((tile * T + r0 < W) & (first > 0), NEG, 0.0)
                x = x + bias
                changed = True
            if changed:
                s_ref[r0 : r0 + STEP, cols] = x
            peak = jnp.maximum(peak, fold(x, jnp.max))
        peak = jnp.max(peak, axis=0, keepdims=True)
        total = jnp.zeros((8, HALF), F32)
        for r0 in starts:
            e = jnp.exp2((s_ref[r0 : r0 + STEP, cols] - peak) * factor)
            s_ref[r0 : r0 + STEP, cols] = e
            total = total + fold(e, jnp.sum)
        inv = 1.0 / jnp.sum(total, axis=0, keepdims=True)
        delta = jnp.zeros((8, HALF), F32)
        for r0 in starts:
            p = (s_ref[r0 : r0 + STEP, cols] * inv).astype(BF16)
            p_ref[r0 : r0 + STEP, cols] = p
            delta = delta + fold(p.astype(F32) * dp_ref[r0 : r0 + STEP, cols], jnp.sum)
        delta = jnp.sum(delta, axis=0, keepdims=True)
        for r0 in starts:
            p = s_ref[r0 : r0 + STEP, cols] * inv
            ds_ref[r0 : r0 + STEP, cols] = (p * (dp_ref[r0 : r0 + STEP, cols] - delta)).astype(BF16)


def attention_kernel(
    scale, tokens, first_ref, lat_ref, q_ref, g_ref, wk_ref, wv_ref, dq_ref, dl_ref,
    ke, ko, v, wko, dke, dko, dve, dvo, acc, rope, se, so, dpe, dpo, pe, po, dse, dso,
):
    pair = pl.program_id(0)
    pairs = pl.num_programs(0)
    first = first_ref[0]
    rows = tokens + W
    dl = wk_ref.shape[1]

    @pl.when(pair == 0)
    def _():
        acc[...] = jnp.zeros_like(acc)
        rope[...] = jnp.zeros_like(rope)
        zero = jnp.zeros((HALF, HALF), BF16)
        for ref in (pe, po, dse, dso):
            ref[SPAN - HALF :, :HALF] = zero
            ref[:HALF, HALF:] = zero
        key_rope = lat_ref[:, dl:]
        ke[:, HALF:] = jnp.concatenate([key_rope, jnp.zeros_like(key_rope)], axis=1)
        wko[...] = jnp.zeros_like(wko)

    wko[:, 64:192] = wk_ref[1]
    wv_pair = jnp.concatenate([wv_ref[0], wv_ref[1]], axis=1)
    for r0 in range(0, rows, 512):
        rr = slice(r0, r0 + 512)
        latent = lat_ref[rr, :dl]
        ke[rr, :HALF] = nn(latent, wk_ref[0]).astype(BF16)
        odd = nn(latent, wko[...]).astype(BF16)
        ko[rr, :HALF] = odd[:, :HALF]
        ko[rr, HALF:] = jnp.concatenate([odd[:, HALF:192], lat_ref[rr, dl:]], axis=1)
        v[rr, :] = nn(latent, wv_pair).astype(BF16)
    for ref in (dke, dko, dve, dvo):
        ref[...] = jnp.zeros_like(ref)

    def tile_step(tile, carry):
        r0 = pl.multiple_of(tile * T, T)
        qs = pl.ds(r0, T)
        ks = pl.ds(r0, SPAN)
        q_e, q_o = q_ref[qs, 0:256], q_ref[qs, 128:384]
        g_e, g_o = g_ref[qs, 0:128], g_ref[qs, 128:256]
        se[...] = nt(ke[ks, :], q_e)
        dpe[...] = nt(v[ks, :HALF], g_e)
        so[...] = nt(ko[ks, :], q_o)
        dpo[...] = nt(v[ks, HALF:], g_o)
        tile_softmax(se, dpe, pe, dse, first, tile, scale)
        dve[ks, :] += nn(pe[...], g_e)
        dke[ks, :] += nn(dse[...], q_e)
        dq_e = tn(dse[...], ke[ks, :])
        tile_softmax(so, dpo, po, dso, first, tile, scale)
        dvo[ks, :] += nn(po[...], g_o)
        dko[ks, :] += nn(dso[...], q_o)
        dq_o = tn(dso[...], ko[ks, :])
        dq_ref[qs, 0:128] = (dq_e[:, :128] * scale).astype(BF16)
        dq_ref[qs, 128:256] = ((dq_e[:, 128:] + dq_o[:, :128]) * scale).astype(BF16)
        dq_ref[qs, 256:384] = (dq_o[:, 128:] * scale).astype(BF16)
        return carry

    lax.fori_loop(0, tokens // T, tile_step, 0)

    lane = lax.broadcasted_iota(jnp.int32, (512, HALF), 1)
    we = jnp.concatenate([wk_ref[0], wv_ref[0]], axis=1)
    for r0 in range(0, rows, 512):
        rr = slice(r0, r0 + 512)
        both = jnp.concatenate(
            [(dke[rr, :HALF] * scale).astype(BF16), dve[rr, :].astype(BF16)], axis=1
        )
        new = nt(both, we)
        new = new + nt((dko[rr, :] * scale).astype(BF16), wko[...])
        new = new + nt(dvo[rr, :].astype(BF16), wv_ref[1])
        acc[rr, :] += new
        rope[rr, :] += jnp.where(lane < 64, dke[rr, HALF:], dko[rr, HALF:])

    @pl.when(pair == pairs - 1)
    def _():
        for r0 in range(0, rows, 512):
            rr = slice(r0, r0 + 512)
            dl_ref[rr, :dl] = acc[rr, :].astype(BF16)
            both = rope[rr, :] * scale
            dl_ref[rr, dl:] = (both[:, :64] + both[:, 64:]).astype(BF16)


def attention(first, latent_ext, queries, grad_out, w_uk, w_uv):
    tokens = queries.shape[0]
    rows, row_dim = latent_ext.shape
    heads, dl, dn = w_uk.shape
    scale = (dn + row_dim - dl) ** -0.5
    vm = pltpu.VMEM
    scratch = (
        [vm((rows, 256), BF16)] * 3
        + [vm((dl, 256), BF16)]
        + [vm((rows, 256), F32)] * 2
        + [vm((rows, 128), F32)] * 2
        + [vm((rows, dl), F32), vm((rows, HALF), F32)]
        + [vm((SPAN, T), F32)] * 4
        + [vm((SPAN, T), BF16)] * 4
    )
    return pl.pallas_call(
        functools.partial(attention_kernel, scale, tokens),
        grid=(heads // 2,),
        in_specs=[
            pl.BlockSpec(memory_space=pltpu.SMEM),
            pl.BlockSpec((rows, row_dim), lambda i: (0, 0)),
            pl.BlockSpec((tokens, 384), lambda i: (0, i)),
            pl.BlockSpec((tokens, 256), lambda i: (0, i)),
            pl.BlockSpec((2, dl, dn), lambda i: (i, 0, 0)),
            pl.BlockSpec((2, dl, dn), lambda i: (i, 0, 0)),
        ],
        out_specs=[
            pl.BlockSpec((tokens, 384), lambda i: (0, i)),
            pl.BlockSpec((rows, row_dim), lambda i: (0, 0)),
        ],
        out_shape=[
            jax.ShapeDtypeStruct(queries.shape, BF16),
            jax.ShapeDtypeStruct((rows, row_dim), BF16),
        ],
        scratch_shapes=scratch,
        compiler_params=pltpu.CompilerParams(
            dimension_semantics=("arbitrary",), vmem_limit_bytes=60 * 1024 * 1024
        ),
        name="attention_backward",
    )(first, latent_ext, queries, grad_out, w_uk, w_uv)


def shards(queries, latent_kv, w_uk, w_uv, grad_out):
    tokens = queries.shape[0]
    row_dim = latent_kv.shape[1]
    ctx, heads = lax.axis_size("ctx"), lax.axis_size("head")
    edge = latent_kv[tokens - W :]
    previous = lax.ppermute(edge, "ctx", [(i, i + 1) for i in range(ctx - 1)])
    latent_ext = jnp.concatenate([previous, latent_kv], axis=0)
    first = (lax.axis_index("ctx") == 0).astype(jnp.int32).reshape(1)
    grad_queries, partial = attention(first, latent_ext, queries, grad_out, w_uk, w_uv)
    own, halo = tokens // heads, W // heads
    pieces = jnp.concatenate(
        [partial[W:].reshape(heads, own, row_dim), partial[:W].reshape(heads, halo, row_dim)], axis=1
    )
    pieces = lax.all_to_all(pieces, "head", 0, 0)
    summed = jnp.sum(pieces.astype(F32), axis=0)
    back = summed[own:]
    low = heads - W // own
    per = own // halo
    parts = []
    for k in range(per):
        pairs = [
            (c * heads + h, (c - 1) * heads + low + h // per)
            for c in range(1, ctx)
            for h in range(k, heads, per)
        ]
        parts.append(lax.ppermute(back, ("ctx", "head"), pairs))
    return grad_queries, summed[:own] + jnp.concatenate(parts, axis=0)


def solution(mesh):
    in_specs = (
        P("ctx", "head"),
        P("ctx", None),
        P("head", None, None),
        P("head", None, None),
        P("ctx", "head"),
    )
    out_specs = (P("ctx", "head"), P(("ctx", "head"), None))
    return jax.shard_map(shards, mesh=mesh, in_specs=in_specs, out_specs=out_specs, check_vma=False)
```

```python
import functools
import math

import jax
import jax.numpy as jnp
from jax import lax
from jax.experimental import pallas as pl
from jax.experimental.pallas import tpu as pltpu
from jax.sharding import Mesh, PartitionSpec as P

W = 512
T = 256
SPAN = T + W
HALF = 128
STEP = 64
TILES = 2
BLOCKS = TILES + 2
ROWS = BLOCKS * T
NEG = -1e30
F32 = jnp.float32
BF16 = jnp.bfloat16


def nn(a, b):
    return lax.dot_general(a, b, (((1,), (0,)), ((), ())), preferred_element_type=F32)


def nt(a, b):
    return lax.dot_general(a, b, (((1,), (1,)), ((), ())), preferred_element_type=F32)


def tn(a, b):
    return lax.dot_general(a, b, (((0,), (0,)), ((), ())), preferred_element_type=F32)


def fold(x, op):
    return op(x.reshape(x.shape[0] // 8, 8, x.shape[1]), axis=0)


def tile_softmax(s_ref, dp_ref, p_ref, ds_ref, tile, halo, bias, scale):
    factor = scale * math.log2(math.e)
    lane = lax.broadcasted_iota(jnp.int32, (STEP, HALF), 1)
    sub = lax.broadcasted_iota(jnp.int32, (STEP, HALF), 0)
    for half in range(2):
        lo = half * HALF
        cols = slice(lo, lo + HALF)
        starts = range(lo, lo + W + HALF, STEP)
        peak = jnp.full((8, HALF), NEG, F32)
        for r0 in starts:
            x = s_ref[r0 : r0 + STEP, cols]
            masked = False
            if r0 < lo + HALF:
                x = jnp.where(sub + (r0 - lo) > lane, x, NEG)
                masked = True
            if r0 >= lo + W:
                x = jnp.where(sub + (r0 - lo - W) <= lane, x, NEG)
                masked = True
            if halo and tile * T + r0 < W:
                x = x + bias
                masked = True
            if masked:
                s_ref[r0 : r0 + STEP, cols] = x
            peak = jnp.maximum(peak, fold(x, jnp.max))
        peak = jnp.max(peak, axis=0, keepdims=True)
        total = jnp.zeros((8, HALF), F32)
        for r0 in starts:
            e = jnp.exp2((s_ref[r0 : r0 + STEP, cols] - peak) * factor)
            s_ref[r0 : r0 + STEP, cols] = e
            total = total + fold(e, jnp.sum)
        inv = 1.0 / jnp.sum(total, axis=0, keepdims=True)
        delta = jnp.zeros((8, HALF), F32)
        for r0 in starts:
            p = (s_ref[r0 : r0 + STEP, cols] * inv).astype(BF16)
            p_ref[half, r0 : r0 + STEP, :] = p
            delta = delta + fold(p.astype(F32) * dp_ref[r0 : r0 + STEP, cols], jnp.sum)
        delta = jnp.sum(delta, axis=0, keepdims=True)
        for r0 in starts:
            p = s_ref[r0 : r0 + STEP, cols] * inv
            d = p * (dp_ref[r0 : r0 + STEP, cols] - delta)
            ds_ref[half, r0 : r0 + STEP, :] = d.astype(BF16)


def wide(ref, rows):
    return jnp.concatenate([ref[0, rows, :], ref[1, rows, :]], axis=1)


def heads_step(scale, halo, bias, lat_rows, q_ref, g_ref, wk_ref, wv_ref, dq_ref, refs):
    (w1, w2, rope, ke, ko, ve, vo, goff, dqmid, acc, rsum, s, dp, p, ds) = refs
    dl = wk_ref.shape[1]
    w1[:, :HALF] = wk_ref[0]
    w1[:, HALF:] = wv_ref[0]
    w2[:, :64] = wv_ref[1, :, 64:]
    w2[:, 64:192] = wk_ref[1]
    w2[:, 192:] = wv_ref[1, :, :64]
    for tile in range(TILES):
        rows = slice(tile * T, tile * T + T)
        goff[rows, :64] = g_ref[rows, 192:256]
        goff[rows, 64:] = g_ref[rows, 128:192]
    lane = lax.broadcasted_iota(jnp.int32, (T, HALF), 1)
    low = lane < 64

    def project(b):
        rr = slice(b * T, b * T + T)
        latent = lat_rows(b)[:, :dl]
        one = nn(latent, w1[...])
        ke[rr, :HALF] = one[:, :HALF].astype(BF16)
        ke[rr, HALF:] = rope[0, rr, :].astype(BF16)
        ve[rr, :] = one[:, HALF:].astype(BF16)
        two = nn(latent, w2[...])
        left, right = two[:, :HALF], two[:, HALF:]
        ko[rr, :HALF] = jnp.where(low, 0.0, left).astype(BF16)
        ko[rr, HALF:] = jnp.where(low, right, rope[1, rr, :]).astype(BF16)
        vo[rr, :] = jnp.where(low, left, right).astype(BF16)

    keys, vals = (ke, ko), (ve, vo)

    def query(h, tile):
        return q_ref[tile * T : tile * T + T, h * HALF : h * HALF + 256]

    def grad(h, tile):
        rows = slice(tile * T, tile * T + T)
        return g_ref[rows, :HALF] if h == 0 else goff[rows, :]

    def scores(h, tile):
        ks = slice(tile * T, tile * T + SPAN)
        s[h][...] = nt(keys[h][ks, :], query(h, tile))
        dp[h][...] = nt(vals[h][ks, :], grad(h, tile))

    def soft(h, tile):
        tile_softmax(s[h], dp[h], p[h][tile], ds[h][tile], tile, halo, bias, scale)

    def query_grad(h, tile):
        rows = slice(tile * T, tile * T + T)
        ks = slice(tile * T, tile * T + SPAN)
        dq = tn(wide(ds[h][tile], slice(0, SPAN)), keys[h][ks, :]) * scale
        if h == 0:
            dq_ref[rows, :HALF] = dq[:, :HALF].astype(BF16)
            dqmid[tile] = dq[:, HALF:]
        else:
            dq_ref[rows, HALF:256] = (dq[:, :HALF] + dqmid[tile]).astype(BF16)
            dq_ref[rows, 256:] = dq[:, HALF:].astype(BF16)

    def key_grad(h, b):
        rr = slice(b * T, b * T + T)
        dk = dv = None
        for tile in range(max(0, b - 2), min(TILES, b + 1)):
            part = slice((b - tile) * T, (b - tile) * T + T)
            a = nn(wide(ds[h][tile], part), query(h, tile))
            c = nn(wide(p[h][tile], part), grad(h, tile))
            dk = a if dk is None else dk + a
            dv = c if dv is None else dv + c
        dk = dk * scale
        left, right = dk[:, :HALF], dk[:, HALF:]
        rsum[h, rr, :] += right
        if h == 1:
            left, right = jnp.where(low, dv, left), jnp.where(low, right, dv)
        else:
            right = dv
        both = jnp.concatenate([left.astype(BF16), right.astype(BF16)], axis=1)
        acc[rr, :] += nt(both, (w1, w2)[h][...])

    last = TILES - 1
    for b in range(last, BLOCKS):
        project(b)
    scores(0, last)
    scores(1, last)
    soft(0, last)
    query_grad(0, last)
    for b in range(last):
        project(b)
    scores(0, 0)
    soft(1, last)
    query_grad(1, last)
    scores(1, 0)
    key_grad(0, BLOCKS - 1)
    key_grad(1, BLOCKS - 1)
    soft(0, 0)
    query_grad(0, 0)
    for b in range(BLOCKS - 1):
        key_grad(0, b)
    soft(1, 0)
    query_grad(1, 0)
    for b in range(BLOCKS - 1):
        key_grad(1, b)


def prepare(lat_rows, dl, refs):
    (_, _, rope, _, _, _, _, _, _, _, rsum, _, _, p, ds) = refs
    rsum[...] = jnp.zeros_like(rsum)
    zero = jnp.zeros((HALF, HALF), BF16)
    for group in (p, ds):
        for head in group:
            for ref in head:
                ref[0, SPAN - HALF :, :] = zero
                ref[1, :HALF, :] = zero
    for b in range(BLOCKS):
        rr = slice(b * T, b * T + T)
        key_rope = lat_rows(b)[:, dl:].astype(F32)
        zeros = jnp.zeros_like(key_rope)
        rope[0, rr, :] = jnp.concatenate([key_rope, zeros], axis=1)
        rope[1, rr, :] = jnp.concatenate([zeros, key_rope], axis=1)


def gather_refs(flat):
    it = iter(flat)
    take = lambda n: [next(it) for _ in range(n)]
    head = take(11)
    s, dp = take(2), take(2)
    p = [take(TILES), take(TILES)]
    ds = [take(TILES), take(TILES)]
    return (*head, s, dp, p, ds)


def near_kernel(scale, lat_ref, q_ref, g_ref, wk_ref, wv_ref, dq_ref, send_ref, keep_ref, *flat):
    refs = gather_refs(flat)
    acc, rsum = refs[9], refs[10]
    dl = wk_ref.shape[1]
    step = pl.program_id(0)
    lat_rows = lambda b: lat_ref[b * T : b * T + T, :]

    @pl.when(step == 0)
    def _():
        prepare(lat_rows, dl, refs)
        acc[...] = jnp.zeros_like(acc)

    heads_step(scale, False, None, lat_rows, q_ref, g_ref, wk_ref, wv_ref, dq_ref, refs)

    @pl.when(step == pl.num_programs(0) - 1)
    def _():
        keep_ref[:, :dl] = acc[:W, :]
        keep_ref[:, dl:] = rsum[0, :W, :64] + rsum[1, :W, 64:]
        per = send_ref.shape[1]
        for k in range(send_ref.shape[0]):
            rr = slice(W + k * per, W + k * per + per)
            send_ref[k, :, :dl] = acc[rr, :].astype(BF16)
            send_ref[k, :, dl:] = (rsum[0, rr, :64] + rsum[1, rr, 64:]).astype(BF16)


def far_kernel(
    scale, info_ref, prev_ref, lat_ref, q_ref, g_ref, wk_ref, wv_ref, kept_ref, _, dq_ref,
    mine_ref, other_ref, *flat
):
    refs = gather_refs(flat)
    acc, rsum = refs[9], refs[10]
    dl = wk_ref.shape[1]
    step = pl.program_id(0)
    bias = jnp.where(info_ref[0] > 0, NEG, 0.0)
    core = info_ref[1]
    half = W // T

    def lat_rows(b):
        ref = prev_ref if b < half else lat_ref
        return ref[b % half * T : b % half * T + T, :]

    @pl.when(step == 0)
    def _():
        prepare(lat_rows, dl, refs)
        acc[:W, :] = jnp.zeros((W, dl), F32)
        acc[W:, :] = kept_ref[:, :dl]
        rsum[0, W:, :64] = kept_ref[:, dl:]

    heads_step(scale, True, bias, lat_rows, q_ref, g_ref, wk_ref, wv_ref, dq_ref, refs)

    @pl.when(step == pl.num_programs(0) - 1)
    def _():
        groups, _, per, _ = mine_ref.shape
        for k in range(groups):
            for part in range(2):
                for ref, which in ((mine_ref, core), (other_ref, 1 - core)):
                    r0 = pl.multiple_of(part * W + (k * 2 + which) * per, per)
                    rr = pl.ds(r0, per)
                    ref[k, part, :, :dl] = acc[rr, :].astype(ref.dtype)
                    turned = rsum[0, rr, :64] + rsum[1, rr, 64:]
                    ref[k, part, :, dl:] = turned.astype(ref.dtype)


def scratch_for(dl):
    vm = pltpu.VMEM
    return (
        [vm((dl, 256), BF16)] * 2
        + [vm((2, ROWS, HALF), F32)]
        + [vm((ROWS, 256), BF16)] * 2
        + [vm((ROWS, HALF), BF16)] * 2
        + [vm((TILES * T, HALF), BF16), vm((TILES, T, HALF), F32)]
        + [vm((ROWS, dl), F32), vm((2, ROWS, HALF), F32)]
        + [vm((SPAN, T), F32)] * 4
        + [vm((2, SPAN, HALF), BF16)] * (4 * TILES)
    )


def params():
    return pltpu.CompilerParams(
        dimension_semantics=("arbitrary",), vmem_limit_bytes=60 * 1024 * 1024
    )


def cost(heads, dl):
    per = 2 * TILES * T * SPAN * 1280 + 2 * ROWS * dl * 256 * 2
    return pl.CostEstimate(
        flops=heads * per, bytes_accessed=8 << 20, transcendentals=heads * TILES * T * SPAN
    )


def near(latent, queries, grad_out, w_uk, w_uv, groups):
    tokens, row_dim = latent.shape
    heads, dl, dn = w_uk.shape
    whole = lambda i: (0, 0)
    return pl.pallas_call(
        functools.partial(near_kernel, (dn + row_dim - dl) ** -0.5),
        grid=(heads // 2,),
        in_specs=[
            pl.BlockSpec((tokens, row_dim), whole),
            pl.BlockSpec((W, 384), lambda i: (1, i)),
            pl.BlockSpec((W, 256), lambda i: (1, i)),
            pl.BlockSpec((2, dl, dn), lambda i: (i, 0, 0)),
            pl.BlockSpec((2, dl, dn), lambda i: (i, 0, 0)),
        ],
        out_specs=[
            pl.BlockSpec((W, 384), lambda i: (1, i)),
            pl.BlockSpec((groups, W // groups, row_dim), lambda i: (0, 0, 0)),
            pl.BlockSpec((W, row_dim), whole),
        ],
        out_shape=[
            jax.ShapeDtypeStruct(queries.shape, BF16),
            jax.ShapeDtypeStruct((groups, W // groups, row_dim), BF16),
            jax.ShapeDtypeStruct((W, row_dim), F32),
        ],
        scratch_shapes=scratch_for(dl),
        compiler_params=params(),
        cost_estimate=cost(heads, dl),
        name="near_rows",
    )(latent, queries, grad_out, w_uk, w_uv)


def far(info, previous, latent, queries, grad_out, w_uk, w_uv, kept, grad_queries, groups):
    row_dim = latent.shape[1]
    heads, dl, dn = w_uk.shape
    per = W // (2 * groups)
    whole = lambda i: (0, 0)
    piece = pl.BlockSpec((groups, 2, per, row_dim), lambda i: (0, 0, 0, 0))
    return pl.pallas_call(
        functools.partial(far_kernel, (dn + row_dim - dl) ** -0.5),
        grid=(heads // 2,),
        in_specs=[
            pl.BlockSpec(memory_space=pltpu.SMEM),
            pl.BlockSpec((W, row_dim), whole),
            pl.BlockSpec((W, row_dim), whole),
            pl.BlockSpec((W, 384), lambda i: (0, i)),
            pl.BlockSpec((W, 256), lambda i: (0, i)),
            pl.BlockSpec((2, dl, dn), lambda i: (i, 0, 0)),
            pl.BlockSpec((2, dl, dn), lambda i: (i, 0, 0)),
            pl.BlockSpec((W, row_dim), whole),
            pl.BlockSpec(memory_space=pl.ANY),
        ],
        out_specs=[pl.BlockSpec((W, 384), lambda i: (0, i)), piece, piece],
        out_shape=[
            jax.ShapeDtypeStruct(queries.shape, BF16),
            jax.ShapeDtypeStruct((groups, 2, per, row_dim), F32),
            jax.ShapeDtypeStruct((groups, 2, per, row_dim), BF16),
        ],
        scratch_shapes=scratch_for(dl),
        input_output_aliases={8: 0},
        compiler_params=params(),
        cost_estimate=cost(heads, dl),
        name="far_rows",
    )(info, previous, latent, queries, grad_out, w_uk, w_uv, kept, grad_queries)


SWAP = [(0, 1), (1, 0)]


def body(queries, latent_kv, w_uk, w_uv, grad_out):
    tokens = queries.shape[0]
    ctx, high, across, cores = (lax.axis_size(a) for a in AXES)
    edge = latent_kv[tokens - W :]
    previous = lax.ppermute(edge, "ctx", [(i, i + 1) for i in range(ctx - 1)])
    core, upper = lax.axis_index("core"), lax.axis_index("yh")
    info = jnp.stack([lax.axis_index("ctx") == 0, core == 1]).astype(jnp.int32)
    grad_queries, send, keep = near(latent_kv, queries, grad_out, w_uk, w_uv, across * cores)
    late = lax.all_to_all(send, ("x", "core"), 0, 0)
    late = jnp.sum(late.astype(F32), axis=0)
    grad_queries, mine, other = far(
        info, previous, latent_kv, queries, grad_out, w_uk, w_uv, keep, grad_queries, across
    )
    to_upper = [(c * high, c * high + 1) for c in range(ctx)]
    from_lower = lax.ppermute(late.astype(BF16), ("ctx", "yh"), to_upper)
    mine = (mine + lax.ppermute(other, "core", SWAP).astype(F32)).astype(BF16)
    part = jnp.sum(lax.all_to_all(mine, "x", 0, 0).astype(F32), axis=0)
    halo, own = part[0], part[1]
    cross = [(c * high + 1, c * high) for c in range(ctx)]
    cross += [(c * high, (c - 1) * high + 1) for c in range(1, ctx)]
    back = [(c * high + 1, (c - 1) * high + 1) for c in range(1, ctx)]
    low16 = halo.astype(BF16)
    mixed = jnp.where(upper == 1, own.astype(BF16), low16)
    got = lax.ppermute(mixed, ("ctx", "yh"), cross).astype(F32)
    got = got + lax.ppermute(low16, ("ctx", "yh"), back).astype(F32)
    got = got + from_lower.astype(F32)
    return grad_queries, jnp.where(upper == 1, late, own) + got


AXES = ("ctx", "yh", "x", "core")


def solution(mesh):
    fine = Mesh(mesh.devices.reshape(mesh.shape["ctx"], 2, 4, 2), AXES)
    head = AXES[1:]
    in_specs = (
        P("ctx", head),
        P("ctx", None),
        P(head, None, None),
        P(head, None, None),
        P("ctx", head),
    )
    out_specs = (P("ctx", head), P(AXES, None))
    return jax.shard_map(body, mesh=fine, in_specs=in_specs, out_specs=out_specs, check_vma=False)
```

```python
import functools
import math

import jax
import jax.numpy as jnp
from jax import lax
from jax.experimental import pallas as pl
from jax.experimental.pallas import tpu as pltpu
from jax.sharding import Mesh, PartitionSpec as P

W = 512
T = 256
SPAN = T + W
HALF = 128
STEP = 64
TILES = 2
BLOCKS = TILES + 2
ROWS = BLOCKS * T
NEG = -1e30
F32 = jnp.float32
BF16 = jnp.bfloat16


def nn(a, b):
    return lax.dot_general(a, b, (((1,), (0,)), ((), ())), preferred_element_type=F32)


def nt(a, b):
    return lax.dot_general(a, b, (((1,), (1,)), ((), ())), preferred_element_type=F32)


def tn(a, b):
    return lax.dot_general(a, b, (((0,), (0,)), ((), ())), preferred_element_type=F32)


def fold(x, op):
    return op(x.reshape(x.shape[0] // 8, 8, x.shape[1]), axis=0)


def tile_softmax(s_ref, dp_ref, p_ref, ds_ref, tile, halo, bias, scale):
    factor = scale * math.log2(math.e)
    lane = lax.broadcasted_iota(jnp.int32, (STEP, HALF), 1)
    sub = lax.broadcasted_iota(jnp.int32, (STEP, HALF), 0)
    for half in range(2):
        lo = half * HALF
        cols = slice(lo, lo + HALF)
        starts = range(lo, lo + W + HALF, STEP)
        peak = jnp.full((8, HALF), NEG, F32)
        for r0 in starts:
            x = s_ref[r0 : r0 + STEP, cols]
            masked = False
            if r0 < lo + HALF:
                x = jnp.where(sub + (r0 - lo) > lane, x, NEG)
                masked = True
            if r0 >= lo + W:
                x = jnp.where(sub + (r0 - lo - W) <= lane, x, NEG)
                masked = True
            if halo and tile * T + r0 < W:
                x = x + bias
                masked = True
            if masked:
                s_ref[r0 : r0 + STEP, cols] = x
            peak = jnp.maximum(peak, fold(x, jnp.max))
        peak = jnp.max(peak, axis=0, keepdims=True)
        total = jnp.zeros((8, HALF), F32)
        for r0 in starts:
            e = jnp.exp2((s_ref[r0 : r0 + STEP, cols] - peak) * factor)
            s_ref[r0 : r0 + STEP, cols] = e
            total = total + fold(e, jnp.sum)
        inv = 1.0 / jnp.sum(total, axis=0, keepdims=True)
        delta = jnp.zeros((8, HALF), F32)
        for r0 in starts:
            p = (s_ref[r0 : r0 + STEP, cols] * inv).astype(BF16)
            p_ref[half, r0 : r0 + STEP, :] = p
            delta = delta + fold(p.astype(F32) * dp_ref[r0 : r0 + STEP, cols], jnp.sum)
        delta = jnp.sum(delta, axis=0, keepdims=True)
        for r0 in starts:
            p = s_ref[r0 : r0 + STEP, cols] * inv
            d = p * (dp_ref[r0 : r0 + STEP, cols] - delta)
            ds_ref[half, r0 : r0 + STEP, :] = d.astype(BF16)


def wide(ref, rows):
    return jnp.concatenate([ref[0, rows, :], ref[1, rows, :]], axis=1)


def heads_step(scale, halo, bias, q_ref, g_ref, wk_ref, wv_ref, dq_ref, refs):
    (w1, w2, lat, rope, ke, ko, ve, vo, goff, dqmid, acc, rsum, s, dp, p, ds) = refs
    w1[:, :HALF] = wk_ref[0]
    w1[:, HALF:] = wv_ref[0]
    w2[:, :64] = wv_ref[1, :, 64:]
    w2[:, 64:192] = wk_ref[1]
    w2[:, 192:] = wv_ref[1, :, :64]
    for tile in range(TILES):
        rows = slice(tile * T, tile * T + T)
        goff[rows, :64] = g_ref[rows, 192:256]
        goff[rows, 64:] = g_ref[rows, 128:192]
    lane = lax.broadcasted_iota(jnp.int32, (T, HALF), 1)
    low = lane < 64

    def project(b):
        rr = slice(b * T, b * T + T)
        latent = lat[rr, :]
        one = nn(latent, w1[...])
        ke[rr, :HALF] = one[:, :HALF].astype(BF16)
        ke[rr, HALF:] = rope[0, rr, :].astype(BF16)
        ve[rr, :] = one[:, HALF:].astype(BF16)
        two = nn(latent, w2[...])
        left, right = two[:, :HALF], two[:, HALF:]
        ko[rr, :HALF] = jnp.where(low, 0.0, left).astype(BF16)
        ko[rr, HALF:] = jnp.where(low, right, rope[1, rr, :]).astype(BF16)
        vo[rr, :] = jnp.where(low, left, right).astype(BF16)

    keys, vals = (ke, ko), (ve, vo)

    def query(h, tile):
        return q_ref[tile * T : tile * T + T, h * HALF : h * HALF + 256]

    def grad(h, tile):
        rows = slice(tile * T, tile * T + T)
        return g_ref[rows, :HALF] if h == 0 else goff[rows, :]

    def scores(h, tile):
        ks = slice(tile * T, tile * T + SPAN)
        s[h][...] = nt(keys[h][ks, :], query(h, tile))
        dp[h][...] = nt(vals[h][ks, :], grad(h, tile))

    def soft(h, tile):
        tile_softmax(s[h], dp[h], p[h][tile], ds[h][tile], tile, halo, bias, scale)

    def query_grad(h, tile):
        rows = slice(tile * T, tile * T + T)
        ks = slice(tile * T, tile * T + SPAN)
        dq = tn(wide(ds[h][tile], slice(0, SPAN)), keys[h][ks, :]) * scale
        if h == 0:
            dq_ref[rows, :HALF] = dq[:, :HALF].astype(BF16)
            dqmid[tile] = dq[:, HALF:]
        else:
            dq_ref[rows, HALF:256] = (dq[:, :HALF] + dqmid[tile]).astype(BF16)
            dq_ref[rows, 256:] = dq[:, HALF:].astype(BF16)

    def key_grad(h, b):
        rr = slice(b * T, b * T + T)
        dk = dv = None
        for tile in range(max(0, b - 2), min(TILES, b + 1)):
            part = slice((b - tile) * T, (b - tile) * T + T)
            a = nn(wide(ds[h][tile], part), query(h, tile))
            c = nn(wide(p[h][tile], part), grad(h, tile))
            dk = a if dk is None else dk + a
            dv = c if dv is None else dv + c
        dk = dk * scale
        left, right = dk[:, :HALF], dk[:, HALF:]
        rsum[h, rr, :] += right
        if h == 1:
            left, right = jnp.where(low, dv, left), jnp.where(low, right, dv)
        else:
            right = dv
        both = jnp.concatenate([left.astype(BF16), right.astype(BF16)], axis=1)
        acc[rr, :] += nt(both, (w1, w2)[h][...])

    last = TILES - 1
    for b in range(last, BLOCKS):
        project(b)
    scores(0, last)
    scores(1, last)
    soft(0, last)
    query_grad(0, last)
    for b in range(last):
        project(b)
    scores(0, 0)
    soft(1, last)
    query_grad(1, last)
    scores(1, 0)
    key_grad(0, BLOCKS - 1)
    key_grad(1, BLOCKS - 1)
    soft(0, 0)
    query_grad(0, 0)
    for b in range(BLOCKS - 1):
        key_grad(0, b)
    soft(1, 0)
    query_grad(1, 0)
    for b in range(BLOCKS - 1):
        key_grad(1, b)


def prepare(lat_cols, refs):
    (_, _, lat, rope, _, _, _, _, _, _, acc, rsum, _, _, p, ds) = refs
    dl = lat.shape[1]
    rsum[...] = jnp.zeros_like(rsum)
    acc[...] = jnp.zeros_like(acc)
    zero = jnp.zeros((HALF, HALF), BF16)
    for group in (p, ds):
        for head in group:
            for ref in head:
                ref[0, SPAN - HALF :, :] = zero
                ref[1, :HALF, :] = zero
    for b in range(BLOCKS):
        rr = slice(b * T, b * T + T)
        cols = lat_cols(b)
        lat[rr, :] = cols[:dl, :].T
        key_rope = cols[dl:, :].astype(F32).T
        zeros = jnp.zeros_like(key_rope)
        rope[0, rr, :] = jnp.concatenate([key_rope, zeros], axis=1)
        rope[1, rr, :] = jnp.concatenate([zeros, key_rope], axis=1)


def gather_refs(flat):
    it = iter(flat)
    take = lambda n: [next(it) for _ in range(n)]
    head = take(12)
    s, dp = take(2), take(2)
    p = [take(TILES), take(TILES)]
    ds = [take(TILES), take(TILES)]
    return (*head, s, dp, p, ds)


def turned(rsum, rr):
    return rsum[0, rr, :64] + rsum[1, rr, 64:]


def near_kernel(
    scale, lat_ref, q_ref, g_ref, wk_ref, wv_ref, dq_ref, mine_ref, other_ref, keep_ref, *flat
):
    refs = gather_refs(flat)
    acc, rsum = refs[10], refs[11]
    dl = wk_ref.shape[1]
    step = pl.program_id(0)
    core = lax.axis_index("core")

    @pl.when(step == 0)
    def _():
        prepare(lambda b: lat_ref[:, b * T : b * T + T], refs)

    heads_step(scale, False, None, q_ref, g_ref, wk_ref, wv_ref, dq_ref, refs)

    @pl.when(step == pl.num_programs(0) - 1)
    def _():
        keep_ref[:, :dl] = acc[:W, :]
        keep_ref[:, dl:] = turned(rsum, slice(0, W))
        groups, per, _ = mine_ref.shape
        for k in range(groups):
            for ref, which in ((mine_ref, core), (other_ref, 1 - core)):
                rr = pl.ds(pl.multiple_of(W + (k * 2 + which) * per, per), per)
                ref[k, :, :dl] = acc[rr, :].astype(BF16)
                ref[k, :, dl:] = turned(rsum, rr).astype(BF16)


def far_kernel(
    scale, prev_ref, lat_ref, q_ref, g_ref, wk_ref, wv_ref, kept_ref, _, dq_ref,
    mine_ref, other_ref, kept, kept_sem, *flat
):
    refs = gather_refs(flat)
    acc, rsum = refs[10], refs[11]
    dl = wk_ref.shape[1]
    step = pl.program_id(0)
    bias = jnp.where(lax.axis_index("ctx") == 0, NEG, 0.0)
    core = lax.axis_index("core")
    half = W // T

    def lat_cols(b):
        ref = prev_ref if b < half else lat_ref
        return ref[:, b % half * T : b % half * T + T]

    @pl.when(step == 0)
    def _():
        pltpu.make_async_copy(kept_ref, kept, kept_sem).start()
        prepare(lat_cols, refs)

    heads_step(scale, True, bias, q_ref, g_ref, wk_ref, wv_ref, dq_ref, refs)

    @pl.when(step == pl.num_programs(0) - 1)
    def _():
        pltpu.make_async_copy(kept_ref, kept, kept_sem).wait()
        groups, _, per, _ = mine_ref.shape
        for k in range(groups):
            for ref, which in ((mine_ref, core), (other_ref, 1 - core)):
                r0 = pl.multiple_of((k * 2 + which) * per, per)
                rr = pl.ds(r0, per)
                ref[k, 0, :, :dl] = acc[rr, :].astype(BF16)
                ref[k, 0, :, dl:] = turned(rsum, rr).astype(BF16)
                own = pl.ds(pl.multiple_of(r0 + W, per), per)
                ref[k, 1, :, :dl] = (acc[own, :] + kept[rr, :dl]).astype(BF16)
                ref[k, 1, :, dl:] = (turned(rsum, own) + kept[rr, dl:]).astype(BF16)


def scratch_for(dl):
    vm = pltpu.VMEM
    return (
        [vm((dl, 256), BF16)] * 2
        + [vm((ROWS, dl), BF16), vm((2, ROWS, HALF), F32)]
        + [vm((ROWS, 256), BF16)] * 2
        + [vm((ROWS, HALF), BF16)] * 2
        + [vm((TILES * T, HALF), BF16), vm((TILES, T, HALF), F32)]
        + [vm((ROWS, dl), F32), vm((2, ROWS, HALF), F32)]
        + [vm((SPAN, T), F32)] * 4
        + [vm((2, SPAN, HALF), BF16)] * (4 * TILES)
    )


def params():
    return pltpu.CompilerParams(
        dimension_semantics=("arbitrary",), vmem_limit_bytes=67043328
    )


def cost(heads, dl):
    per = 2 * TILES * T * SPAN * 1280 + 2 * ROWS * dl * 256 * 2
    return pl.CostEstimate(
        flops=heads * per, bytes_accessed=8 << 20, transcendentals=heads * TILES * T * SPAN
    )


def near(latent, queries, grad_out, w_uk, w_uv, groups):
    row_dim, tokens = latent.shape
    heads, dl, dn = w_uk.shape
    per = W // (2 * groups)
    whole = lambda i: (0, 0)
    piece = pl.BlockSpec((groups, per, row_dim), lambda i: (0, 0, 0))
    return pl.pallas_call(
        functools.partial(near_kernel, (dn + row_dim - dl) ** -0.5),
        grid=(heads // 2,),
        in_specs=[
            pl.BlockSpec((row_dim, tokens), whole),
            pl.BlockSpec((W, 384), lambda i: (1, i)),
            pl.BlockSpec((W, 256), lambda i: (1, i)),
            pl.BlockSpec((2, dl, dn), lambda i: (i, 0, 0)),
            pl.BlockSpec((2, dl, dn), lambda i: (i, 0, 0)),
        ],
        out_specs=[
            pl.BlockSpec((W, 384), lambda i: (1, i)), piece, piece,
            pl.BlockSpec((W, row_dim), whole),
        ],
        out_shape=[
            jax.ShapeDtypeStruct(queries.shape, BF16),
            jax.ShapeDtypeStruct((groups, per, row_dim), BF16),
            jax.ShapeDtypeStruct((groups, per, row_dim), BF16),
            jax.ShapeDtypeStruct((W, row_dim), F32),
        ],
        scratch_shapes=scratch_for(dl),
        compiler_params=params(),
        cost_estimate=cost(heads, dl),
        name="near_rows",
    )(latent, queries, grad_out, w_uk, w_uv)


def far(previous, latent, queries, grad_out, w_uk, w_uv, kept, grad_queries, groups):
    row_dim = latent.shape[0]
    heads, dl, dn = w_uk.shape
    per = W // (2 * groups)
    whole = lambda i: (0, 0)
    piece = pl.BlockSpec((groups, 2, per, row_dim), lambda i: (0, 0, 0, 0))
    return pl.pallas_call(
        functools.partial(far_kernel, (dn + row_dim - dl) ** -0.5),
        grid=(heads // 2,),
        in_specs=[
            pl.BlockSpec((row_dim, W), whole),
            pl.BlockSpec((row_dim, W), whole),
            pl.BlockSpec((W, 384), lambda i: (0, i)),
            pl.BlockSpec((W, 256), lambda i: (0, i)),
            pl.BlockSpec((2, dl, dn), lambda i: (i, 0, 0)),
            pl.BlockSpec((2, dl, dn), lambda i: (i, 0, 0)),
            pl.BlockSpec(memory_space=pl.ANY),
            pl.BlockSpec(memory_space=pl.ANY),
        ],
        out_specs=[pl.BlockSpec((W, 384), lambda i: (0, i)), piece, piece],
        out_shape=[
            jax.ShapeDtypeStruct(queries.shape, BF16),
            jax.ShapeDtypeStruct((groups, 2, per, row_dim), BF16),
            jax.ShapeDtypeStruct((groups, 2, per, row_dim), BF16),
        ],
        scratch_shapes=[pltpu.VMEM((W, row_dim), F32), pltpu.SemaphoreType.DMA(())]
        + scratch_for(dl),
        input_output_aliases={7: 0},
        compiler_params=params(),
        cost_estimate=cost(heads, dl),
        name="far_rows",
    )(previous, latent, queries, grad_out, w_uk, w_uv, kept, grad_queries)


SWAP = [(0, 1), (1, 0)]
AXES = ("ctx", "yh", "x", "core")


def pick(array, *chunks):
    parts = [lax.dynamic_index_in_dim(array, k, 0, keepdims=False) for k in chunks]
    return parts[0] if len(parts) == 1 else jnp.stack(parts)


def halve(array, mirror_first):
    x = lax.axis_index("x")
    near_by = ([(k, k ^ 1) for k in range(4)], lambda k: k ^ 1)
    mirror = ([(k, 3 - k) for k in range(4)], lambda k: 3 - k)
    first, second = (mirror, near_by) if mirror_first else (near_by, mirror)
    peer = first[1](x)
    got = lax.ppermute(pick(array, peer, second[1](peer)).astype(BF16), "x", first[0])
    held = pick(array, x, second[1](x)) + got.astype(F32)
    return held[0] + lax.ppermute(held[1].astype(BF16), "x", second[0]).astype(F32)


def body(queries, latent_kv, w_uk, w_uv, grad_out):
    latent = latent_kv.T
    tokens = latent.shape[1]
    ctx, high, across, _ = (lax.axis_size(a) for a in AXES)
    upper = lax.axis_index("yh") == 1
    edge = latent[:, tokens - W :]
    previous = lax.ppermute(edge, "ctx", [(i, i + 1) for i in range(ctx - 1)])
    grad_queries, late_mine, late_other, keep = near(
        latent, queries, grad_out, w_uk, w_uv, across
    )
    late_got = lax.ppermute(late_other, "core", SWAP)
    grad_queries, mine, other = far(
        previous, latent, queries, grad_out, w_uk, w_uv, keep, grad_queries, across
    )
    got = lax.ppermute(other, "core", SWAP)
    late = late_mine.astype(F32) + late_got.astype(F32)
    total = jnp.concatenate([late[:, None], mine.astype(F32) + got.astype(F32)], axis=1)
    mid = total.shape[2] // 2
    part = jnp.concatenate(
        [halve(total[:, :, :mid], False), halve(total[:, :, mid:], True)], axis=1
    )
    late, halo, own = part[0], part[1], part[2]
    halo = halo.astype(BF16)
    swap = [(c * high + k, c * high + 1 - k) for c in range(ctx) for k in range(2)]
    cross = [(c * high, (c - 1) * high + 1) for c in range(1, ctx)]
    back = [(c * high + 1, (c - 1) * high + 1) for c in range(1, ctx)]
    got = lax.ppermute(jnp.where(upper, own, late).astype(BF16), ("ctx", "yh"), swap).astype(F32)
    got = got + lax.ppermute(halo, ("ctx", "yh"), cross).astype(F32)
    got = got + lax.ppermute(halo, ("ctx", "yh"), back).astype(F32)
    return grad_queries, jnp.where(upper, late, own) + got


def solution(mesh):
    fine = Mesh(mesh.devices.reshape(mesh.shape["ctx"], 2, 4, 2), AXES)
    head = AXES[1:]
    in_specs = (
        P("ctx", head),
        P("ctx", None),
        P(head, None, None),
        P(head, None, None),
        P("ctx", head),
    )
    out_specs = (P("ctx", head), P(AXES, None))
    return jax.shard_map(body, mesh=fine, in_specs=in_specs, out_specs=out_specs, check_vma=False)
```

```python
import functools
import math

import jax
import jax.numpy as jnp
from jax import lax
from jax.experimental import pallas as pl
from jax.experimental.pallas import tpu as pltpu
from jax.sharding import Mesh, PartitionSpec as P

W = 512
T = 256
SPAN = T + W
HALF = 128
STEP = 64
TILES = 2
BLOCKS = TILES + 2
ROWS = BLOCKS * T
SHARED = W // T
NEG = -1e30
F32 = jnp.float32
BF16 = jnp.bfloat16


def nn(a, b):
    return lax.dot_general(a, b, (((1,), (0,)), ((), ())), preferred_element_type=F32)


def nt(a, b):
    return lax.dot_general(a, b, (((1,), (1,)), ((), ())), preferred_element_type=F32)


def tn(a, b):
    return lax.dot_general(a, b, (((0,), (0,)), ((), ())), preferred_element_type=F32)


def fold(x, op):
    return op(x.reshape(x.shape[0] // 8, 8, x.shape[1]), axis=0)


def tile_softmax(s_ref, dp_ref, p_ref, ds_ref, tile, halo, bias, scale):
    factor = scale * math.log2(math.e)
    lane = lax.broadcasted_iota(jnp.int32, (STEP, HALF), 1)
    sub = lax.broadcasted_iota(jnp.int32, (STEP, HALF), 0)
    for half in range(2):
        lo = half * HALF
        cols = slice(lo, lo + HALF)
        starts = range(lo, lo + W + HALF, STEP)
        peak = jnp.full((8, HALF), NEG, F32)
        for r0 in starts:
            x = s_ref[r0 : r0 + STEP, cols]
            masked = False
            if r0 < lo + HALF:
                x = jnp.where(sub + (r0 - lo) > lane, x, NEG)
                masked = True
            if r0 >= lo + W:
                x = jnp.where(sub + (r0 - lo - W) <= lane, x, NEG)
                masked = True
            if halo and tile * T + r0 < W:
                x = x + bias
                masked = True
            if masked:
                s_ref[r0 : r0 + STEP, cols] = x
            peak = jnp.maximum(peak, fold(x, jnp.max))
        peak = jnp.max(peak, axis=0, keepdims=True)
        total = jnp.zeros((8, HALF), F32)
        for r0 in starts:
            e = jnp.exp2((s_ref[r0 : r0 + STEP, cols] - peak) * factor)
            s_ref[r0 : r0 + STEP, cols] = e
            total = total + fold(e, jnp.sum)
        inv = 1.0 / jnp.sum(total, axis=0, keepdims=True)
        delta = jnp.zeros((8, HALF), F32)
        for r0 in starts:
            p = (s_ref[r0 : r0 + STEP, cols] * inv).astype(BF16)
            p_ref[half, r0 : r0 + STEP, :] = p
            delta = delta + fold(p.astype(F32) * dp_ref[r0 : r0 + STEP, cols], jnp.sum)
        delta = jnp.sum(delta, axis=0, keepdims=True)
        for r0 in starts:
            p = s_ref[r0 : r0 + STEP, cols] * inv
            d = p * (dp_ref[r0 : r0 + STEP, cols] - delta)
            ds_ref[half, r0 : r0 + STEP, :] = d.astype(BF16)


def wide(ref, rows):
    return jnp.concatenate([ref[0, rows, :], ref[1, rows, :]], axis=1)


def heads_step(scale, halo, bias, q_ref, g_ref, wk_ref, wv_ref, dq_ref, kv_ref, x_ref, refs):
    (w1, w2, lat, rope, ke, ko, ve, vo, goff, dqmid, acc, rsum, s, dp, p, ds) = refs
    w1[:, :HALF] = wk_ref[0]
    w1[:, HALF:] = wv_ref[0]
    w2[:, :64] = wv_ref[1, :, 64:]
    w2[:, 64:192] = wk_ref[1]
    w2[:, 192:] = wv_ref[1, :, :64]
    for tile in range(TILES):
        rows = slice(tile * T, tile * T + T)
        goff[rows, :64] = g_ref[rows, 192:256]
        goff[rows, 64:] = g_ref[rows, 128:192]
    lane = lax.broadcasted_iota(jnp.int32, (T, HALF), 1)
    low = lane < 64

    def project(b):
        rr = slice(b * T, b * T + T)
        latent = lat[rr, :]
        one = nn(latent, w1[...])
        ke[rr, :HALF] = one[:, :HALF].astype(BF16)
        ke[rr, HALF:] = rope[0, rr, :].astype(BF16)
        ve[rr, :] = one[:, HALF:].astype(BF16)
        two = nn(latent, w2[...])
        left, right = two[:, :HALF], two[:, HALF:]
        ko[rr, :HALF] = jnp.where(low, 0.0, left).astype(BF16)
        ko[rr, HALF:] = jnp.where(low, right, rope[1, rr, :]).astype(BF16)
        vo[rr, :] = jnp.where(low, left, right).astype(BF16)
        if not halo and b < SHARED:
            for ref, cols in shared:
                kv_ref[rr, cols] = ref[rr, :]

    def obtain(b):
        if not halo or b < SHARED:
            project(b)

    def span(which, tile):
        ref, cols = shared[which]
        start, stop = tile * T, tile * T + SPAN
        if not halo or stop <= W:
            return ref[start:stop, :]
        return jnp.concatenate([ref[start:W, :], kv_ref[: stop - W, cols]], axis=0)

    shared = (
        (ke, slice(0, 256)),
        (ko, slice(256, 512)),
        (ve, slice(512, 640)),
        (vo, slice(640, 768)),
    )

    def query(h, tile):
        return q_ref[tile * T : tile * T + T, h * HALF : h * HALF + 256]

    def grad(h, tile):
        rows = slice(tile * T, tile * T + T)
        return g_ref[rows, :HALF] if h == 0 else goff[rows, :]

    def scores(h, tile):
        s[h][...] = nt(span(h, tile), query(h, tile))
        dp[h][...] = nt(span(2 + h, tile), grad(h, tile))

    def soft(h, tile):
        tile_softmax(s[h], dp[h], p[h][tile], ds[h][tile], tile, halo, bias, scale)

    def query_grad(h, tile):
        rows = slice(tile * T, tile * T + T)
        dq = tn(wide(ds[h][tile], slice(0, SPAN)), span(h, tile)) * scale
        if h == 0:
            dq_ref[rows, :HALF] = dq[:, :HALF].astype(BF16)
            dqmid[tile] = dq[:, HALF:]
        else:
            dq_ref[rows, HALF:256] = (dq[:, :HALF] + dqmid[tile]).astype(BF16)
            dq_ref[rows, 256:] = dq[:, HALF:].astype(BF16)

    def key_grad(h, b):
        rr = slice(b * T, b * T + T)
        dk = dv = None
        for tile in range(max(0, b - 2), min(TILES, b + 1)):
            part = slice((b - tile) * T, (b - tile) * T + T)
            a = nn(wide(ds[h][tile], part), query(h, tile))
            c = nn(wide(p[h][tile], part), grad(h, tile))
            dk = a if dk is None else dk + a
            dv = c if dv is None else dv + c
        dk = dk * scale
        left, right = dk[:, :HALF], dk[:, HALF:]
        rsum[h, rr, :] += right
        if h == 1:
            left, right = jnp.where(low, dv, left), jnp.where(low, right, dv)
        else:
            right = dv
        both = jnp.concatenate([left, right], axis=1)
        cols = slice(h * 256, h * 256 + 256)
        if not halo and b < SHARED:
            x_ref[rr, cols] = both.astype(BF16)
            return
        if halo and b >= SHARED:
            both = both + x_ref[b % SHARED * T : b % SHARED * T + T, cols].astype(F32)
        acc[rr, :] += nt(both.astype(BF16), (w1, w2)[h][...])

    last = TILES - 1
    for b in range(last, BLOCKS):
        obtain(b)
    scores(0, last)
    scores(1, last)
    soft(0, last)
    query_grad(0, last)
    for b in range(last):
        obtain(b)
    scores(0, 0)
    soft(1, last)
    query_grad(1, last)
    scores(1, 0)
    key_grad(0, BLOCKS - 1)
    key_grad(1, BLOCKS - 1)
    soft(0, 0)
    query_grad(0, 0)
    for b in range(BLOCKS - 1):
        key_grad(0, b)
    soft(1, 0)
    query_grad(1, 0)
    for b in range(BLOCKS - 1):
        key_grad(1, b)


def prepare(lat_cols, blocks, refs):
    (_, _, lat, rope, _, _, _, _, _, _, acc, rsum, _, _, p, ds) = refs
    dl = lat.shape[1]
    rsum[...] = jnp.zeros_like(rsum)
    acc[...] = jnp.zeros_like(acc)
    zero = jnp.zeros((HALF, HALF), BF16)
    for group in (p, ds):
        for head in group:
            for ref in head:
                ref[0, SPAN - HALF :, :] = zero
                ref[1, :HALF, :] = zero
    for b in range(blocks):
        rr = slice(b * T, b * T + T)
        cols = lat_cols(b)
        lat[rr, :] = cols[:dl, :].T
        key_rope = cols[dl:, :].astype(F32).T
        zeros = jnp.zeros_like(key_rope)
        rope[0, rr, :] = jnp.concatenate([key_rope, zeros], axis=1)
        rope[1, rr, :] = jnp.concatenate([zeros, key_rope], axis=1)


def gather_refs(flat):
    it = iter(flat)
    take = lambda n: [next(it) for _ in range(n)]
    head = take(12)
    s, dp = take(2), take(2)
    p = [take(TILES), take(TILES)]
    ds = [take(TILES), take(TILES)]
    return (*head, s, dp, p, ds)


def turned(rsum, rr):
    return rsum[0, rr, :64] + rsum[1, rr, 64:]


def near_kernel(
    scale, lat_ref, q_ref, g_ref, wk_ref, wv_ref, dq_ref, mine_ref, other_ref, keep_ref,
    kv_ref, x_ref, *flat
):
    refs = gather_refs(flat)
    acc, rsum = refs[10], refs[11]
    dl = wk_ref.shape[1]
    step = pl.program_id(0)
    core = lax.axis_index("core")

    @pl.when(step == 0)
    def _():
        prepare(lambda b: lat_ref[:, b * T : b * T + T], BLOCKS, refs)

    heads_step(scale, False, None, q_ref, g_ref, wk_ref, wv_ref, dq_ref, kv_ref, x_ref, refs)

    @pl.when(step == pl.num_programs(0) - 1)
    def _():
        keep_ref[...] = turned(rsum, slice(0, W))
        groups, per, _ = mine_ref.shape
        for k in range(groups):
            for ref, which in ((mine_ref, core), (other_ref, 1 - core)):
                rr = pl.ds(pl.multiple_of(W + (k * 2 + which) * per, per), per)
                ref[k, :, :dl] = acc[rr, :].astype(BF16)
                ref[k, :, dl:] = turned(rsum, rr).astype(BF16)


def far_kernel(
    scale, prev_ref, q_ref, g_ref, wk_ref, wv_ref, kept_ref, kv_ref, x_ref, _, dq_ref,
    mine_ref, other_ref, *flat
):
    refs = gather_refs(flat)
    acc, rsum = refs[10], refs[11]
    dl = wk_ref.shape[1]
    step = pl.program_id(0)
    bias = jnp.where(lax.axis_index("ctx") == 0, NEG, 0.0)
    core = lax.axis_index("core")

    @pl.when(step == 0)
    def _():
        prepare(lambda b: prev_ref[:, b * T : b * T + T], SHARED, refs)

    heads_step(scale, True, bias, q_ref, g_ref, wk_ref, wv_ref, dq_ref, kv_ref, x_ref, refs)

    @pl.when(step == pl.num_programs(0) - 1)
    def _():
        groups, _, per, _ = mine_ref.shape
        for k in range(groups):
            for ref, which in ((mine_ref, core), (other_ref, 1 - core)):
                r0 = pl.multiple_of((k * 2 + which) * per, per)
                rr = pl.ds(r0, per)
                ref[k, 0, :, :dl] = acc[rr, :].astype(BF16)
                ref[k, 0, :, dl:] = turned(rsum, rr).astype(BF16)
                own = pl.ds(pl.multiple_of(r0 + W, per), per)
                ref[k, 1, :, :dl] = acc[own, :].astype(BF16)
                ref[k, 1, :, dl:] = (turned(rsum, own) + kept_ref[rr, :]).astype(BF16)


def scratch_for(dl):
    vm = pltpu.VMEM
    return (
        [vm((dl, 256), BF16)] * 2
        + [vm((ROWS, dl), BF16), vm((2, ROWS, HALF), F32)]
        + [vm((ROWS, 256), BF16)] * 2
        + [vm((ROWS, HALF), BF16)] * 2
        + [vm((TILES * T, HALF), BF16), vm((TILES, T, HALF), F32)]
        + [vm((ROWS, dl), F32), vm((2, ROWS, HALF), F32)]
        + [vm((SPAN, T), F32)] * 4
        + [vm((2, SPAN, HALF), BF16)] * (4 * TILES)
    )


def params():
    return pltpu.CompilerParams(
        dimension_semantics=("arbitrary",), vmem_limit_bytes=67043328
    )


def cost(heads, dl):
    per = 2 * TILES * T * SPAN * 1280 + 2 * ROWS * dl * 256 * 2
    return pl.CostEstimate(
        flops=heads * per, bytes_accessed=8 << 20, transcendentals=heads * TILES * T * SPAN
    )


def near(latent, queries, grad_out, w_uk, w_uv, groups):
    row_dim, tokens = latent.shape
    heads, dl, dn = w_uk.shape
    per = W // (2 * groups)
    whole = lambda i: (0, 0)
    piece = pl.BlockSpec((groups, per, row_dim), lambda i: (0, 0, 0))
    return pl.pallas_call(
        functools.partial(near_kernel, (dn + row_dim - dl) ** -0.5),
        grid=(heads // 2,),
        in_specs=[
            pl.BlockSpec((row_dim, tokens), whole),
            pl.BlockSpec((W, 384), lambda i: (1, i)),
            pl.BlockSpec((W, 256), lambda i: (1, i)),
            pl.BlockSpec((2, dl, dn), lambda i: (i, 0, 0)),
            pl.BlockSpec((2, dl, dn), lambda i: (i, 0, 0)),
        ],
        out_specs=[
            pl.BlockSpec((W, 384), lambda i: (1, i)), piece, piece,
            pl.BlockSpec((W, row_dim - dl), whole),
            pl.BlockSpec((W, 768), lambda i: (0, i)),
            pl.BlockSpec((W, 512), lambda i: (0, i)),
        ],
        out_shape=[
            jax.ShapeDtypeStruct(queries.shape, BF16),
            jax.ShapeDtypeStruct((groups, per, row_dim), BF16),
            jax.ShapeDtypeStruct((groups, per, row_dim), BF16),
            jax.ShapeDtypeStruct((W, row_dim - dl), F32),
            jax.ShapeDtypeStruct((W, heads // 2 * 768), BF16),
            jax.ShapeDtypeStruct((W, heads // 2 * 512), BF16),
        ],
        scratch_shapes=scratch_for(dl),
        compiler_params=params(),
        cost_estimate=cost(heads, dl),
        name="near_rows",
    )(latent, queries, grad_out, w_uk, w_uv)


def far(previous, queries, grad_out, w_uk, w_uv, kept, grad_queries, groups):
    kept, keys_values, shared_rows = kept
    row_dim = previous.shape[0]
    heads, dl, dn = w_uk.shape
    per = W // (2 * groups)
    whole = lambda i: (0, 0)
    piece = pl.BlockSpec((groups, 2, per, row_dim), lambda i: (0, 0, 0, 0))
    return pl.pallas_call(
        functools.partial(far_kernel, (dn + row_dim - dl) ** -0.5),
        grid=(heads // 2,),
        in_specs=[
            pl.BlockSpec((row_dim, W), whole),
            pl.BlockSpec((W, 384), lambda i: (0, i)),
            pl.BlockSpec((W, 256), lambda i: (0, i)),
            pl.BlockSpec((2, dl, dn), lambda i: (i, 0, 0)),
            pl.BlockSpec((2, dl, dn), lambda i: (i, 0, 0)),
            pl.BlockSpec((W, row_dim - dl), whole),
            pl.BlockSpec((W, 768), lambda i: (0, i)),
            pl.BlockSpec((W, 512), lambda i: (0, i)),
            pl.BlockSpec(memory_space=pl.ANY),
        ],
        out_specs=[pl.BlockSpec((W, 384), lambda i: (0, i)), piece, piece],
        out_shape=[
            jax.ShapeDtypeStruct(queries.shape, BF16),
            jax.ShapeDtypeStruct((groups, 2, per, row_dim), BF16),
            jax.ShapeDtypeStruct((groups, 2, per, row_dim), BF16),
        ],
        scratch_shapes=scratch_for(dl),
        input_output_aliases={8: 0},
        compiler_params=params(),
        cost_estimate=cost(heads, dl),
        name="far_rows",
    )(previous, queries, grad_out, w_uk, w_uv, kept, keys_values, shared_rows, grad_queries)


SWAP = [(0, 1), (1, 0)]
AXES = ("ctx", "yh", "x", "core")


def pick(array, *chunks):
    parts = [lax.dynamic_index_in_dim(array, k, 0, keepdims=False) for k in chunks]
    return parts[0] if len(parts) == 1 else jnp.stack(parts)


def halve(array, mirror_first):
    x = lax.axis_index("x")
    near_by = ([(k, k ^ 1) for k in range(4)], lambda k: k ^ 1)
    mirror = ([(k, 3 - k) for k in range(4)], lambda k: 3 - k)
    first, second = (mirror, near_by) if mirror_first else (near_by, mirror)
    peer = first[1](x)
    got = lax.ppermute(pick(array, peer, second[1](peer)).astype(BF16), "x", first[0])
    held = pick(array, x, second[1](x)) + got.astype(F32)
    return held[0] + lax.ppermute(held[1].astype(BF16), "x", second[0]).astype(F32)


def body(queries, latent_kv, w_uk, w_uv, grad_out):
    latent = latent_kv.T
    tokens = latent.shape[1]
    ctx, high, across, _ = (lax.axis_size(a) for a in AXES)
    upper = lax.axis_index("yh") == 1
    edge = latent[:, tokens - W :]
    previous = lax.ppermute(edge, "ctx", [(i, i + 1) for i in range(ctx - 1)])
    grad_queries, late_mine, late_other, *keep = near(
        latent, queries, grad_out, w_uk, w_uv, across
    )
    late_got = lax.ppermute(late_other, "core", SWAP)
    grad_queries, mine, other = far(
        previous, queries, grad_out, w_uk, w_uv, keep, grad_queries, across
    )
    got = lax.ppermute(other, "core", SWAP)
    late = late_mine.astype(F32) + late_got.astype(F32)
    total = jnp.concatenate([late[:, None], mine.astype(F32) + got.astype(F32)], axis=1)
    mid = total.shape[2] // 2
    part = jnp.concatenate(
        [halve(total[:, :, :mid], False), halve(total[:, :, mid:], True)], axis=1
    )
    late, halo, own = part[0], part[1], part[2]
    halo = halo.astype(BF16)
    swap = [(c * high + k, c * high + 1 - k) for c in range(ctx) for k in range(2)]
    cross = [(c * high, (c - 1) * high + 1) for c in range(1, ctx)]
    back = [(c * high + 1, (c - 1) * high + 1) for c in range(1, ctx)]
    got = lax.ppermute(jnp.where(upper, own, late).astype(BF16), ("ctx", "yh"), swap).astype(F32)
    got = got + lax.ppermute(halo, ("ctx", "yh"), cross).astype(F32)
    got = got + lax.ppermute(halo, ("ctx", "yh"), back).astype(F32)
    return grad_queries, jnp.where(upper, late, own) + got


def solution(mesh):
    fine = Mesh(mesh.devices.reshape(mesh.shape["ctx"], 2, 4, 2), AXES)
    head = AXES[1:]
    in_specs = (
        P("ctx", head),
        P("ctx", None),
        P(head, None, None),
        P(head, None, None),
        P("ctx", head),
    )
    out_specs = (P("ctx", head), P(AXES, None))
    return jax.shard_map(body, mesh=fine, in_specs=in_specs, out_specs=out_specs, check_vma=False)
```
